32 devices in a mesh: row: 8 (over y, x, core), col: 4 (over z).
Axes of the slice: x: 2, y: 2, z: 4, core: 2. Of those that a mesh axis runs over, the one named last changes fastest.
Arguments:
- points: bfloat16 [16, 16384], P(None, ('row', 'col')), may hold values from -6 to 6
- spread: bfloat16 [16384], P(('row', 'col')), may hold values from 2 to 12
- vectors: bfloat16 [8, 16384], P(None, ('row', 'col')), may hold values from -6 to 6
Outputs:
- basis: float32 [8, 16384], P(None, ('row', 'col'))
The draws below stay inside these ranges and needn't reach their ends.
All inputs are finite; a program needn't handle non-finite values.
Results may differ from the reference program's by a relative error of at most 0.012.
Values may be sent and summed in bfloat16 or wider, within the bound.
No kernel may reach another device: no remote copies, remote signals or barrier semaphores. Data moves between devices by JAX's collectives and lax.ppermute only.
A program may use at most 64 MiB of HBM per device.

```python
import math
import jax
import jax.numpy as jnp
from jax import lax

DIM = 16
KVEC = 8
NPTS = 16384


def shard_levels(stream_key, extent, shards, least, largest):
    factor_of, own = 1.0, jax.random.fold_in(stream_key, 6)
    for position, blocks in shards:
        heights = jnp.exp(jax.random.uniform(jax.random.fold_in(own, position), (blocks,), jnp.float32, least / len(shards), largest / len(shards)))
        factor_of = factor_of * jnp.repeat(heights, extent[position] // blocks).reshape([-1 if axis == position else 1 for axis in range(len(extent))])
    return factor_of


def gaussian(rng, dims, width, reach, shards=(), dtype=jnp.bfloat16):
    drawn = jax.random.normal(rng, dims, jnp.float32) * width
    if len(shards) > 0:
        drawn = shard_levels(rng, dims, shards, -0.22, 0.18) * drawn
    return jnp.clip(drawn, min=-reach, max=reach).astype(dtype)


def setup_inputs(seed: int = 0) -> dict:
    splits = jax.random.split(jax.random.key(seed), 4)
    return {
        "points": gaussian(splits[0], (DIM, NPTS), 1.0, 6.0, ((1, 32),)),
        "spread": jnp.clip(jnp.exp(math.log(12.0) - 1.7917595 * jax.random.uniform(splits[1], (NPTS,), jnp.float32) ** shard_levels(splits[1], (NPTS,), ((0, 32),), -0.2, 0.2)), 2.0, 12.0).astype(jnp.bfloat16),
        "vectors": gaussian(splits[2], (KVEC, NPTS), 1.0, 6.0, ((1, 32),)),
    }


def reference(points, spread, vectors):
    count = points.shape[1]
    ones_row = jnp.ones((1, count), jnp.bfloat16)
    extended = jnp.concatenate([vectors, ones_row], axis=0)
    sqnorm = lax.optimization_barrier(jnp.sum(points.astype(jnp.float32) * points.astype(jnp.float32), axis=0))
    scales = spread.astype(jnp.float32)
    block = math.gcd(count, 512)
    nblocks = count // block
    row_pts = jnp.transpose(points.reshape(points.shape[0], nblocks, block), (1, 0, 2))
    row_norm = sqnorm.reshape(nblocks, block)
    row_scale = scales.reshape(nblocks, block)

    def one_block(operands):
        pts_blk, norm_blk, scale_blk = operands
        cross = lax.dot_general(pts_blk.astype(jnp.float32), points.astype(jnp.float32), (((0,), (0,)), ((), ())), preferred_element_type=jnp.float32)
        dist = norm_blk[:, None] + sqnorm[None, :] - 2.0 * cross
        affinity = jnp.exp(-dist / (scale_blk[:, None] * scales[None, :])).astype(jnp.bfloat16)
        return lax.dot_general(extended.astype(jnp.float32), affinity.astype(jnp.float32), (((1,), (1,)), ((), ())), preferred_element_type=jnp.float32)
    parts = lax.map(one_block, (row_pts, row_norm, row_scale))
    product = jnp.transpose(parts, (1, 0, 2)).reshape(extended.shape[0], count)
    kvec = vectors.shape[0]
    update = product[:kvec] / product[kvec:kvec + 1]
    gram = lax.optimization_barrier(jnp.sum(update[:, None, :] * update[None, :, :], axis=2))
    lower = jnp.linalg.cholesky(gram)
    solved = lax.linalg.triangular_solve(lower, update, left_side=True, lower=True)
    return jnp.sqrt(jnp.float32(count)) * solved
```

```python
import functools
import math

import jax
import jax.numpy as jnp
from jax import lax
from jax.experimental import pallas as pl
from jax.experimental.pallas import tpu as pltpu
from jax.sharding import PartitionSpec as P


VMEM = pl.BlockSpec(memory_space=pltpu.VMEM)
F32 = jnp.float32
BF16 = jnp.bfloat16
AUX = 8
ONE, SCALE = 3, 4


def call(kernel, out_shape, *args, scratch=(), flops=10**6, moved=10**5, exps=0):
    return pl.pallas_call(
        kernel,
        out_shape=out_shape,
        in_specs=[VMEM] * len(args),
        out_specs=jax.tree.map(lambda _: VMEM, out_shape),
        scratch_shapes=scratch,
        cost_estimate=pl.CostEstimate(flops=flops, bytes_accessed=moved, transcendentals=exps),
    )(*args)


def three_parts(x):
    hi = x.astype(BF16).astype(F32)
    rest = x - hi
    mid = rest.astype(BF16).astype(F32)
    return hi, mid, rest - mid


def pack_kernel(points_ref, spread_ref, vectors_ref, out_ref):
    pts = points_ref[...].astype(F32)
    local = pts.shape[1]
    norm = jnp.sum(pts * pts, axis=0, keepdims=True)
    row = lax.broadcasted_iota(jnp.int32, (AUX, local), 0)
    aux = jnp.zeros((AUX, local), F32)
    entries = (*three_parts(norm), jnp.ones_like(norm), spread_ref[...].astype(F32))
    for place, entry in enumerate(entries):
        aux = jnp.where(row == place, entry, aux)
    packed = jnp.concatenate([pts, aux, vectors_ref[...].astype(F32)], axis=0)
    out_ref[...] = packed.astype(BF16)


def left_factor(block, dims):
    rows = block.astype(F32)
    at = lambda i: rows[dims + i : dims + i + 1]
    rate = F32(math.log2(math.e)) / at(SCALE)
    norm = at(0) + at(1) + at(2)
    row = lax.broadcasted_iota(jnp.int32, (AUX, rows.shape[1]), 0)
    aux = jnp.where(row < ONE, -rate, jnp.where(row == ONE, -norm * rate, F32(0)))
    factor = jnp.concatenate(
        [2 * rate * rows[:dims], aux, jnp.zeros((rows.shape[0] - dims - AUX, rows.shape[1]), F32)], axis=0
    )
    parts = three_parts(factor)
    return jnp.concatenate([*parts, jnp.zeros_like(factor)], axis=0)


def accumulate(left_ref, block_ref, acc_ref, dims, wide, tall):
    rows, width = left_ref.shape[0], block_ref.shape[1]

    def step(c, carry):
        block = block_ref[:, pl.ds(pl.multiple_of(c * wide, wide), wide)]
        right = jnp.concatenate([block] * 4, axis=0)
        scale = block[dims : dims + 2 * AUX].astype(F32)[SCALE : SCALE + 1]
        rate = 1.0 / scale
        for m in range(0, rows, tall):
            exponent = lax.dot_general(
                left_ref[m : m + tall, :], right, (((1,), (0,)), ((), ())), preferred_element_type=F32
            )
            affinity = jnp.exp2(exponent * rate).astype(BF16)
            acc_ref[:, m : m + tall] += lax.dot_general(
                block, affinity, (((1,), (1,)), ((), ())), preferred_element_type=F32
            )
        return carry

    lax.fori_loop(0, width // wide, step, 0)


def near_kernel(dims, wide, tall, own_ref, mate_ref, group_ref, left_ref, acc_ref):
    local = own_ref.shape[1]
    left_ref[:local, :] = left_factor(own_ref[...], dims).T.astype(BF16)
    left_ref[local:, :] = left_factor(mate_ref[...], dims).T.astype(BF16)
    acc_ref[...] = jnp.zeros_like(acc_ref)
    accumulate(left_ref, group_ref, acc_ref, dims, wide, tall)


def far_kernel(dims, wide, tall, left_ref, part_ref, *refs):
    *group_refs, out_ref, acc_ref = refs
    acc_ref[...] = part_ref[...]
    for group_ref in group_refs:
        accumulate(left_ref, group_ref, acc_ref, dims, wide, tall)
    out_ref[...] = acc_ref[dims:, :]


def update_kernel(mine_ref, other_ref, update_ref, gram_ref):
    local = update_ref.shape[1]
    own = mine_ref[:, :local] + other_ref[:, local:]
    mate = mine_ref[:, local:] + other_ref[:, :local]
    own = own[AUX:] / own[ONE : ONE + 1]
    mate = mate[AUX:] / mate[ONE : ONE + 1]
    update_ref[...] = own
    kvec = own.shape[0]
    column = lax.broadcasted_iota(jnp.int32, gram_ref.shape, 1)
    gram = jnp.zeros(gram_ref.shape, F32)
    for k in range(kvec):
        with_k = jnp.sum(own * own[k : k + 1] + mate * mate[k : k + 1], axis=1, keepdims=True)
        gram = jnp.where(column == k, with_k, gram)
    gram_ref[...] = gram


def basis_kernel(root, update_ref, *refs):
    *gram_refs, out_ref = refs
    gram = functools.reduce(lambda a, b: a + b, [ref[...] for ref in gram_refs])
    rest = update_ref[...]
    kvec = rest.shape[0]
    row = lax.broadcasted_iota(jnp.int32, gram.shape, 0)
    column = lax.broadcasted_iota(jnp.int32, gram.shape, 1)
    for k in range(kvec - 1):
        factor = jnp.where(row[:, :1] > k, gram[:, k : k + 1] / gram[k : k + 1, k : k + 1], F32(0))
        rest = rest - factor * rest[k : k + 1]
        gram = gram - factor * gram[k : k + 1]
    pivot = jnp.sum(jnp.where(row == column, gram, F32(0)), axis=1, keepdims=True)
    out_ref[...] = rest * (root / jnp.sqrt(pivot))


def partners(count, step):
    if count & (count - 1) == 0:
        return [i ^ step for i in range(count)]
    return [(i + step) % count for i in range(count)]


def shards(points, spread, vectors):
    n_row, n_col = lax.axis_size("row"), lax.axis_size("col")
    dims, local = points.shape
    kvec = vectors.shape[0]
    packed = dims + AUX + kvec
    chips = n_row // 2

    def to_mate(x):
        return lax.ppermute(x, "row", [(i, i ^ 1) for i in range(n_row)])

    def along(x):
        return [
            lax.ppermute(x, "col", list(enumerate(partners(n_col, step)))) for step in range(1, n_col)
        ]

    def across(x):
        return [
            lax.ppermute(
                x, "row", [(2 * i + core, 2 * j + core) for i, j in enumerate(partners(chips, step)) for core in (0, 1)]
            )
            for step in range(1, chips)
        ]

    shape = jax.ShapeDtypeStruct
    block = call(pack_kernel, shape((packed, local), BF16), points, spread.reshape(1, local), vectors)
    mate = to_mate(block)
    group = jnp.concatenate([block, *along(block)], axis=1)
    far = across(group)

    wide, tall = math.gcd(n_col * local, 1024), math.gcd(2 * local, 256)
    size = dict(
        flops=2 * 2 * local * n_col * local * 160, exps=2 * local * n_col * local, moved=10**6
    )
    left, part = call(
        functools.partial(near_kernel, dims, wide, tall),
        (shape((2 * local, 4 * packed), BF16), shape((packed, 2 * local), F32)),
        block, mate, group, **size,
    )
    part = call(
        functools.partial(far_kernel, dims, wide, tall),
        shape((packed - dims, 2 * local), F32),
        left, part, *far,
        scratch=[pltpu.VMEM((packed, 2 * local), F32)],
        **{k: v * (chips - 1) for k, v in size.items()},
    )
    update, gram = call(
        update_kernel, (shape((kvec, local), F32), shape((kvec, 128), F32)), part, to_mate(part)
    )
    gram = functools.reduce(lambda a, b: a + b, along(gram), gram)
    root = math.sqrt(local * n_row * n_col)
    return call(
        functools.partial(basis_kernel, root), shape((kvec, local), F32), update, gram, *across(gram)
    )


def solution(mesh):
    in_specs = (P(None, ("row", "col")), P(("row", "col")), P(None, ("row", "col")))
    out_specs = P(None, ("row", "col"))
    return jax.shard_map(shards, mesh=mesh, in_specs=in_specs, out_specs=out_specs, check_vma=False)
```

```python
import functools
import math

import jax
import jax.numpy as jnp
from jax import lax
from jax.experimental import pallas as pl
from jax.experimental.pallas import tpu as pltpu
from jax.sharding import PartitionSpec as P


VMEM = pl.BlockSpec(memory_space=pltpu.VMEM)
F32 = jnp.float32
BF16 = jnp.bfloat16
AUX = 8
ONE, SCALE = 3, 4


def call(kernel, out_shape, *args, scratch=(), out_vmem=True, in_hbm=False, flops=10**6, moved=10**5, exps=0, limit=16 * 2**20):
    return pl.pallas_call(
        kernel,
        out_shape=jax.tree.map(lambda s: pltpu.VMEM(s.shape, s.dtype), out_shape) if out_vmem else out_shape,
        in_specs=[VMEM] * len(args),
        out_specs=jax.tree.map(lambda _: VMEM, out_shape),
        scratch_shapes=scratch,
        cost_estimate=pl.CostEstimate(flops=flops, bytes_accessed=moved, transcendentals=exps),
        compiler_params=pltpu.CompilerParams(vmem_limit_bytes=limit),
    )(*[pltpu.with_memory_space_constraint(x, pltpu.HBM if in_hbm else pltpu.VMEM) for x in args])


def three_parts(x):
    hi = x.astype(BF16).astype(F32)
    rest = x - hi
    mid = rest.astype(BF16).astype(F32)
    return hi, mid, rest - mid


def pack_kernel(points_ref, spread_ref, vectors_ref, out_ref):
    pts = points_ref[...].astype(F32)
    local = pts.shape[1]
    norm = jnp.sum(pts * pts, axis=0, keepdims=True)
    row = lax.broadcasted_iota(jnp.int32, (AUX, local), 0)
    aux = jnp.zeros((AUX, local), F32)
    entries = (*three_parts(norm), jnp.ones_like(norm), spread_ref[...].reshape(1, local).astype(F32))
    for place, entry in enumerate(entries):
        aux = jnp.where(row == place, entry, aux)
    packed = jnp.concatenate([pts, aux, vectors_ref[...].astype(F32)], axis=0)
    out_ref[...] = packed.astype(BF16)


def left_factor(block, dims):
    rows = block.astype(F32)
    at = lambda i: rows[dims + i : dims + i + 1]
    rate = F32(math.log2(math.e)) / at(SCALE)
    norm = at(0) + at(1) + at(2)
    row = lax.broadcasted_iota(jnp.int32, (AUX, rows.shape[1]), 0)
    aux = jnp.where(row < ONE, -rate, jnp.where(row == ONE, -norm * rate, F32(0)))
    factor = jnp.concatenate(
        [2 * rate * rows[:dims], aux, jnp.zeros((rows.shape[0] - dims - AUX, rows.shape[1]), F32)], axis=0
    )
    parts = three_parts(factor)
    return jnp.concatenate([*parts, jnp.zeros_like(factor)], axis=0)


def accumulate(left_ref, block_ref, acc_ref, dims, wide, tall):
    rows, width = left_ref.shape[0], block_ref.shape[1]

    def step(c, carry):
        block = block_ref[:, pl.ds(pl.multiple_of(c * wide, wide), wide)]
        right = jnp.concatenate([block] * 4, axis=0)
        scale = block[dims : dims + 2 * AUX].astype(F32)[SCALE : SCALE + 1]
        rate = 1.0 / scale
        for m in range(0, rows, tall):
            exponent = lax.dot_general(
                left_ref[m : m + tall, :], right, (((1,), (0,)), ((), ())), preferred_element_type=F32
            )
            affinity = jnp.exp2(exponent * rate).astype(BF16)
            acc_ref[:, m : m + tall] += lax.dot_general(
                block, affinity, (((1,), (1,)), ((), ())), preferred_element_type=F32
            )
        return carry

    lax.fori_loop(0, width // wide, step, 0)


def own_kernel(dims, wide, tall, own_ref, mate_ref, left_ref, acc_ref):
    local = own_ref.shape[1]
    left_ref[:local, :] = left_factor(own_ref[...], dims).T.astype(BF16)
    left_ref[local:, :] = left_factor(mate_ref[...], dims).T.astype(BF16)
    acc_ref[...] = jnp.zeros_like(acc_ref)
    accumulate(left_ref, own_ref, acc_ref, dims, wide, tall)


def add_kernel(dims, wide, tall, left_ref, part_ref, *refs):
    *block_refs, acc_ref = refs
    acc_ref[...] = part_ref[...]
    for block_ref in block_refs:
        accumulate(left_ref, block_ref, acc_ref, dims, wide, tall)


def last_kernel(dims, wide, tall, left_ref, part_ref, *refs):
    *block_refs, out_ref, acc_ref = refs
    add_kernel(dims, wide, tall, left_ref, part_ref, *block_refs, acc_ref)
    out_ref[...] = acc_ref[dims:, :]


def join_kernel(*refs):
    *block_refs, out_ref = refs
    at = 0
    for block_ref in block_refs:
        out_ref[:, at : at + block_ref.shape[1]] = block_ref[...]
        at += block_ref.shape[1]


def sum_kernel(*refs):
    *part_refs, out_ref = refs
    out_ref[...] = functools.reduce(lambda a, b: a + b, [ref[...] for ref in part_refs])


def update_kernel(mine_ref, other_ref, update_ref, gram_ref):
    local = update_ref.shape[1]
    own = mine_ref[:, :local] + other_ref[:, local:]
    mate = mine_ref[:, local:] + other_ref[:, :local]
    own = own[AUX:] / own[ONE : ONE + 1]
    mate = mate[AUX:] / mate[ONE : ONE + 1]
    update_ref[...] = own
    kvec = own.shape[0]
    column = lax.broadcasted_iota(jnp.int32, gram_ref.shape, 1)
    gram = jnp.zeros(gram_ref.shape, F32)
    for k in range(kvec):
        with_k = jnp.sum(own * own[k : k + 1] + mate * mate[k : k + 1], axis=1, keepdims=True)
        gram = jnp.where(column == k, with_k, gram)
    gram_ref[...] = gram


def basis_kernel(root, update_ref, *refs):
    *gram_refs, out_ref = refs
    gram = functools.reduce(lambda a, b: a + b, [ref[...] for ref in gram_refs])
    rest = update_ref[...]
    kvec = rest.shape[0]
    row = lax.broadcasted_iota(jnp.int32, gram.shape, 0)
    column = lax.broadcasted_iota(jnp.int32, gram.shape, 1)
    for k in range(kvec - 1):
        factor = jnp.where(row[:, :1] > k, gram[:, k : k + 1] / gram[k : k + 1, k : k + 1], F32(0))
        rest = rest - factor * rest[k : k + 1]
        gram = gram - factor * gram[k : k + 1]
    pivot = jnp.sum(jnp.where(row == column, gram, F32(0)), axis=1, keepdims=True)
    out_ref[...] = rest * (root / jnp.sqrt(pivot))


def partners(count, step):
    if count & (count - 1) == 0:
        return [i ^ step for i in range(count)]
    return [(i + step) % count for i in range(count)]


def shards(points, spread, vectors):
    n_row, n_col = lax.axis_size("row"), lax.axis_size("col")
    dims, local = points.shape
    kvec = vectors.shape[0]
    packed = dims + AUX + kvec
    chips = n_row // 2

    def to_mate(x):
        return lax.ppermute(x, "row", [(i, i ^ 1) for i in range(n_row)])

    def along(x):
        return [
            lax.ppermute(x, "col", list(enumerate(partners(n_col, step)))) for step in range(1, n_col)
        ]

    def across(x):
        return [
            lax.ppermute(
                x, "row", [(2 * i + core, 2 * j + core) for i, j in enumerate(partners(chips, step)) for core in (0, 1)]
            )
            for step in range(1, chips)
        ]

    shape = jax.ShapeDtypeStruct
    block = call(pack_kernel, shape((packed, local), BF16), points, spread, vectors, in_hbm=True)
    mate = to_mate(block)
    column = along(block)
    beside = across(block)

    wide, tall = math.gcd(local, 512), math.gcd(2 * local, 1024)

    def size(blocks):
        pairs = 2 * local * blocks * local
        return dict(flops=2 * 2 * pairs * 160, exps=pairs, moved=10**6)

    left, part = call(
        functools.partial(own_kernel, dims, wide, tall),
        (shape((2 * local, 4 * packed), BF16), shape((packed, 2 * local), F32)),
        block, mate, **size(1),
    )
    column, left, part = lax.optimization_barrier((column, left, part))
    joined = call(join_kernel, shape((packed, local * (n_col - 1)), BF16), *column)
    far = across(joined)
    near = [*column, *beside]
    part = call(
        functools.partial(add_kernel, dims, wide, tall),
        shape((packed, 2 * local), F32), left, part, *near, **size(len(near)),
    )
    part = call(
        functools.partial(last_kernel, dims, wide, tall),
        shape((packed - dims, 2 * local), F32),
        left, part, *far,
        scratch=[pltpu.VMEM((packed, 2 * local), F32)],
        **size(len(far) * (n_col - 1)),
    )
    update, gram = call(
        update_kernel, (shape((kvec, local), F32), shape((kvec, 128), F32)), part, to_mate(part)
    )
    gram = call(sum_kernel, shape(gram.shape, F32), gram, *along(gram))
    root = math.sqrt(local * n_row * n_col)
    return call(
        functools.partial(basis_kernel, root), shape((kvec, local), F32), update, gram, *across(gram), out_vmem=False
    )


def solution(mesh):
    in_specs = (P(None, ("row", "col")), P(("row", "col")), P(None, ("row", "col")))
    out_specs = P(None, ("row", "col"))
    return jax.shard_map(shards, mesh=mesh, in_specs=in_specs, out_specs=out_specs, check_vma=False)
```

```python
import functools
import math

import jax
import jax.numpy as jnp
from jax import lax
from jax.experimental import pallas as pl
from jax.experimental.pallas import tpu as pltpu
from jax.sharding import PartitionSpec as P


VMEM = pl.BlockSpec(memory_space=pltpu.VMEM)
F32 = jnp.float32
BF16 = jnp.bfloat16
AUX = 8
ONE, SCALE = 3, 4


def call(kernel, out_shape, *args, scratch=(), out_vmem=True, in_hbm=False, flops=10**6, moved=10**5, exps=0, limit=16 * 2**20):
    return pl.pallas_call(
        kernel,
        out_shape=jax.tree.map(lambda s: pltpu.VMEM(s.shape, s.dtype), out_shape) if out_vmem else out_shape,
        in_specs=[VMEM] * len(args),
        out_specs=jax.tree.map(lambda _: VMEM, out_shape),
        scratch_shapes=scratch,
        cost_estimate=pl.CostEstimate(flops=flops, bytes_accessed=moved, transcendentals=exps),
        compiler_params=pltpu.CompilerParams(vmem_limit_bytes=limit),
    )(*[pltpu.with_memory_space_constraint(x, pltpu.HBM if in_hbm else pltpu.VMEM) for x in args])


def three_parts(x):
    hi = x.astype(BF16).astype(F32)
    rest = x - hi
    mid = rest.astype(BF16).astype(F32)
    return hi, mid, rest - mid


def span_of(dims, kvec, local):
    return (dims + kvec) // AUX * local + 128 * (-(-local // (128 * AUX)))


def pack_kernel(points_ref, spread_ref, vectors_ref, out_ref):
    local = points_ref.shape[1]
    at = 0
    for ref in (points_ref, vectors_ref):
        for top in range(0, ref.shape[0], AUX):
            out_ref[:, at : at + local] = ref[top : top + AUX, :]
            at += local
    spread = spread_ref[...].reshape(1, local).astype(F32)
    for column in range(0, local, 128 * AUX):
        pieces = [spread[:, i : i + 128] for i in range(column, min(local, column + 128 * AUX), 128)]
        out_ref[:, at : at + 128] = place_rows(pieces, 128).astype(BF16)
        at += 128


def place_rows(entries, width):
    row = lax.broadcasted_iota(jnp.int32, (AUX, width), 0)
    out = jnp.ones((AUX, width), F32)
    for place, entry in enumerate(entries):
        out = jnp.where(row == place, entry, out)
    return out


def expand(ref, at, dims, kvec, local):
    groups = [
        ref[:, pl.ds(at + i * local, local)].astype(F32) for i in range((dims + kvec) // AUX)
    ]
    points = jnp.concatenate(groups[: dims // AUX], axis=0)
    base = at + len(groups) * local
    spread = []
    for i in range(local // 128):
        tile = ref[:, pl.ds(base + i // AUX * 128, 128)].astype(F32)
        spread.append(tile[i % AUX : i % AUX + 1])
    norm = jnp.sum(points * points, axis=0, keepdims=True)
    aux = place_rows((*three_parts(norm), jnp.ones_like(norm), jnp.concatenate(spread, axis=1)), local)
    return jnp.concatenate([points, aux, *groups[dims // AUX :]], axis=0)


def left_factor(rows, dims):
    at = lambda i: rows[dims + i : dims + i + 1]
    rate = F32(math.log2(math.e)) / at(SCALE)
    norm = at(0) + at(1) + at(2)
    row = lax.broadcasted_iota(jnp.int32, (AUX, rows.shape[1]), 0)
    aux = jnp.where(row < ONE, -rate, jnp.where(row == ONE, -norm * rate, F32(0)))
    factor = jnp.concatenate(
        [2 * rate * rows[:dims], aux, jnp.zeros((rows.shape[0] - dims - AUX, rows.shape[1]), F32)], axis=0
    )
    parts = three_parts(factor)
    return jnp.concatenate([*parts, jnp.zeros_like(factor)], axis=0)


def accumulate(left_ref, block_ref, acc_ref, sizes, tall):
    dims, _, _ = sizes
    rows, span = left_ref.shape[0], span_of(*sizes)
    count = block_ref.shape[1] // span

    def step(c, carry):
        full = expand(block_ref, pl.multiple_of(c * span, 128), *sizes)
        rate = 1.0 / full[dims + SCALE : dims + SCALE + 1]
        block = full.astype(BF16)
        right = jnp.concatenate([block] * 4, axis=0)
        for m in range(0, rows, tall):
            exponent = lax.dot_general(
                left_ref[m : m + tall, :], right, (((1,), (0,)), ((), ())), preferred_element_type=F32
            )
            affinity = jnp.exp2(exponent * rate).astype(BF16)
            acc_ref[:, m : m + tall] += lax.dot_general(
                block, affinity, (((1,), (1,)), ((), ())), preferred_element_type=F32
            )
        return carry

    if count == 1:
        step(0, 0)
    else:
        lax.fori_loop(0, count, step, 0, unroll=min(count, 3))


def own_kernel(sizes, tall, own_ref, mate_ref, left_ref, acc_ref):
    dims, _, local = sizes
    left_ref[:local, :] = left_factor(expand(own_ref, 0, *sizes), dims).T.astype(BF16)
    left_ref[local:, :] = left_factor(expand(mate_ref, 0, *sizes), dims).T.astype(BF16)
    acc_ref[...] = jnp.zeros_like(acc_ref)

    @pl.when(lax.axis_index("row") % 2 == 1)
    def _():
        accumulate(left_ref, own_ref, acc_ref, sizes, tall)
        accumulate(left_ref, mate_ref, acc_ref, sizes, tall)


def add_kernel(sizes, tall, left_ref, part_ref, *refs):
    *block_refs, acc_ref = refs
    acc_ref[...] = part_ref[...]
    for block_ref in block_refs:
        accumulate(left_ref, block_ref, acc_ref, sizes, tall)


def last_kernel(sizes, tall, left_ref, part_ref, *refs):
    *block_refs, out_ref, acc_ref = refs
    add_kernel(sizes, tall, left_ref, part_ref, *block_refs, acc_ref)
    out_ref[...] = acc_ref[sizes[0] :, :]


def join_kernel(*refs):
    *block_refs, out_ref = refs
    at = 0
    for block_ref in block_refs:
        out_ref[:, at : at + block_ref.shape[1]] = block_ref[...]
        at += block_ref.shape[1]


def sum_kernel(*refs):
    *part_refs, out_ref = refs
    out_ref[...] = functools.reduce(lambda a, b: a + b, [ref[...] for ref in part_refs])


def update_kernel(mine_ref, other_ref, update_ref, gram_ref):
    local = update_ref.shape[1]
    own = mine_ref[:, :local] + other_ref[:, local:]
    mate = mine_ref[:, local:] + other_ref[:, :local]
    own = own[AUX:] / own[ONE : ONE + 1]
    mate = mate[AUX:] / mate[ONE : ONE + 1]
    update_ref[...] = own
    kvec = own.shape[0]
    column = lax.broadcasted_iota(jnp.int32, gram_ref.shape, 1)
    gram = jnp.zeros(gram_ref.shape, F32)
    for k in range(kvec):
        with_k = jnp.sum(own * own[k : k + 1] + mate * mate[k : k + 1], axis=1, keepdims=True)
        gram = jnp.where(column == k, with_k, gram)
    gram_ref[...] = gram


def basis_kernel(root, update_ref, *refs):
    *gram_refs, out_ref = refs
    gram = functools.reduce(lambda a, b: a + b, [ref[...] for ref in gram_refs])
    rest = update_ref[...]
    kvec = rest.shape[0]
    row = lax.broadcasted_iota(jnp.int32, gram.shape, 0)
    column = lax.broadcasted_iota(jnp.int32, gram.shape, 1)
    for k in range(kvec - 1):
        factor = jnp.where(row[:, :1] > k, gram[:, k : k + 1] / gram[k : k + 1, k : k + 1], F32(0))
        rest = rest - factor * rest[k : k + 1]
        gram = gram - factor * gram[k : k + 1]
    pivot = jnp.sum(jnp.where(row == column, gram, F32(0)), axis=1, keepdims=True)
    out_ref[...] = rest * (root / jnp.sqrt(pivot))


def partners(count, step):
    if count & (count - 1) == 0:
        return [i ^ step for i in range(count)]
    return [(i + step) % count for i in range(count)]


def step(points, spread, vectors):
    n_row, n_col = lax.axis_size("row"), lax.axis_size("col")
    dims, local = points.shape
    kvec = vectors.shape[0]
    packed = dims + AUX + kvec
    sizes = (dims, kvec, local)
    span = span_of(*sizes)
    chips = n_row // 2

    def to_mate(x):
        return lax.ppermute(x, "row", [(i, i ^ 1) for i in range(n_row)])

    def along(x):
        return [lax.ppermute(x, "col", list(enumerate(partners(n_col, step)))) for step in range(1, n_col)]

    def across(x):
        return [
            lax.ppermute(
                x, "row", [(2 * i + core, 2 * j + core) for i, j in enumerate(partners(chips, step)) for core in (0, 1)]
            )
            for step in range(1, chips)
        ]

    shape = jax.ShapeDtypeStruct
    block = call(pack_kernel, shape((AUX, span), BF16), points, spread, vectors, in_hbm=True)
    mate = to_mate(block)
    column = along(block)
    beside = across(block)

    tall = math.gcd(2 * local, 1024)

    def size(blocks):
        pairs = 2 * local * blocks * local
        return dict(flops=2 * 2 * pairs * 160, exps=pairs, moved=10**6)

    left, part = call(
        functools.partial(own_kernel, sizes, tall),
        (shape((2 * local, 4 * packed), BF16), shape((packed, 2 * local), F32)),
        block, mate, **size(1),
    )
    column, left, part = lax.optimization_barrier((column, left, part))
    joined = call(join_kernel, shape((AUX, span * (n_col - 1)), BF16), *column)
    far = across(joined)
    near = [*column, *beside]
    part = call(
        functools.partial(add_kernel, sizes, tall),
        shape((packed, 2 * local), F32), left, part, *near, **size(len(near)),
    )
    for index, block in enumerate(far[::-1]):
        final = index == len(far) - 1
        part = call(
            functools.partial(last_kernel if final else add_kernel, sizes, tall),
            shape((packed - dims if final else packed, 2 * local), F32),
            left, part, block,
            scratch=[pltpu.VMEM((packed, 2 * local), F32)] * final,
            **size(n_col - 1),
        )
    update, gram = call(update_kernel, (shape((kvec, local), F32), shape((kvec, 128), F32)), part, to_mate(part))
    gram = call(sum_kernel, shape(gram.shape, F32), gram, *along(gram))
    root = math.sqrt(local * n_row * n_col)
    return call(
        functools.partial(basis_kernel, root), shape((kvec, local), F32), update, gram, *across(gram), out_vmem=False
    )


def solution(mesh):
    in_specs = (P(None, ("row", "col")), P(("row", "col")), P(None, ("row", "col")))
    out_specs = P(None, ("row", "col"))
    return jax.shard_map(step, mesh=mesh, in_specs=in_specs, out_specs=out_specs, check_vma=False)
```

```python
import functools
import math

import jax
import jax.numpy as jnp
from jax import lax
from jax.experimental import pallas as pl
from jax.experimental.pallas import tpu as pltpu
from jax.sharding import PartitionSpec as P


VMEM = pl.BlockSpec(memory_space=pltpu.VMEM)
F32 = jnp.float32
BF16 = jnp.bfloat16
AUX = 8
ONE, SCALE = 3, 4


def call(kernel, out_shape, *args, scratch=(), out_vmem=True, in_hbm=False, flops=10**6, moved=10**5, exps=0, limit=16 * 2**20):
    return pl.pallas_call(
        kernel,
        out_shape=jax.tree.map(lambda s: pltpu.VMEM(s.shape, s.dtype), out_shape) if out_vmem else out_shape,
        in_specs=[VMEM] * len(args),
        out_specs=jax.tree.map(lambda _: VMEM, out_shape),
        scratch_shapes=scratch,
        cost_estimate=pl.CostEstimate(flops=flops, bytes_accessed=moved, transcendentals=exps),
        compiler_params=pltpu.CompilerParams(vmem_limit_bytes=limit),
    )(*[pltpu.with_memory_space_constraint(x, pltpu.HBM if in_hbm else pltpu.VMEM) for x in args])


def three_parts(x):
    hi = x.astype(BF16).astype(F32)
    rest = x - hi
    mid = rest.astype(BF16).astype(F32)
    return hi, mid, rest - mid


def span_of(dims, kvec, local):
    return (dims + kvec) // AUX * local + 128 * (-(-local // (128 * AUX)))


def pack_kernel(points_ref, spread_ref, vectors_ref, out_ref):
    local = points_ref.shape[1]
    at = 0
    for ref in (points_ref, vectors_ref):
        for top in range(0, ref.shape[0], AUX):
            out_ref[:, at : at + local] = ref[top : top + AUX, :]
            at += local
    spread = spread_ref[...].reshape(1, local).astype(F32)
    for column in range(0, local, 128 * AUX):
        pieces = [spread[:, i : i + 128] for i in range(column, min(local, column + 128 * AUX), 128)]
        out_ref[:, at : at + 128] = place_rows(pieces, 128).astype(BF16)
        at += 128


def place_rows(entries, width):
    row = lax.broadcasted_iota(jnp.int32, (AUX, width), 0)
    out = jnp.ones((AUX, width), F32)
    for place, entry in enumerate(entries):
        out = jnp.where(row == place, entry, out)
    return out


def expand(ref, at, dims, kvec, local):
    groups = [
        ref[:, pl.ds(at + i * local, local)].astype(F32) for i in range((dims + kvec) // AUX)
    ]
    points = jnp.concatenate(groups[: dims // AUX], axis=0)
    base = at + len(groups) * local
    spread = []
    for i in range(local // 128):
        tile = ref[:, pl.ds(base + i // AUX * 128, 128)].astype(F32)
        spread.append(tile[i % AUX : i % AUX + 1])
    norm = jnp.sum(points * points, axis=0, keepdims=True)
    aux = place_rows((*three_parts(norm), jnp.ones_like(norm), jnp.concatenate(spread, axis=1)), local)
    return jnp.concatenate([points, aux, *groups[dims // AUX :]], axis=0)


def left_factor(rows, dims):
    at = lambda i: rows[dims + i : dims + i + 1]
    rate = F32(math.log2(math.e)) / at(SCALE)
    norm = at(0) + at(1) + at(2)
    row = lax.broadcasted_iota(jnp.int32, (AUX, rows.shape[1]), 0)
    aux = jnp.where(row < ONE, -rate, jnp.where(row == ONE, -norm * rate, F32(0)))
    factor = jnp.concatenate(
        [2 * rate * rows[:dims], aux, jnp.zeros((rows.shape[0] - dims - AUX, rows.shape[1]), F32)], axis=0
    )
    parts = three_parts(factor)
    return jnp.concatenate([*parts, jnp.zeros_like(factor)], axis=0)


def accumulate(left_ref, block_ref, acc_ref, sizes, tall):
    dims, _, _ = sizes
    rows, span = left_ref.shape[0], span_of(*sizes)
    count = block_ref.shape[1] // span

    def step(c, carry):
        full = expand(block_ref, pl.multiple_of(c * span, 128), *sizes)
        rate = 1.0 / full[dims + SCALE : dims + SCALE + 1]
        block = full.astype(BF16)
        right = jnp.concatenate([block] * 3, axis=0)
        for m in range(0, rows, tall):
            exponent = lax.dot_general(
                left_ref[m : m + tall, : right.shape[0]], right, (((1,), (0,)), ((), ())), preferred_element_type=F32
            )
            affinity = jnp.exp2(exponent * rate).astype(BF16)
            acc_ref[:, m : m + tall] += lax.dot_general(
                block[dims:], affinity, (((1,), (1,)), ((), ())), preferred_element_type=F32
            )
        return carry

    if count == 1:
        step(0, 0)
    else:
        lax.fori_loop(0, count, step, 0, unroll=min(count, 3))


def set_left(left_ref, at, block_refs, sizes):
    dims, _, local = sizes
    for ref, start in block_refs:
        factor = left_factor(expand(ref, start, *sizes), dims)
        left_ref[at : at + local, :] = factor.T.astype(BF16)
        at += local


def own_kernel(sizes, tall, own_ref, mate_ref, left_ref, acc_ref):
    set_left(left_ref, 0, [(own_ref, 0), (mate_ref, 0)], sizes)
    acc_ref[...] = jnp.zeros_like(acc_ref)
    accumulate(left_ref, own_ref, acc_ref, sizes, tall)


def buddy_kernel(sizes, tall, own_ref, mate_ref, buddy_ref, upper_ref, part_ref, left_ref, acc_ref, half_ref, sum_ref):
    rows = upper_ref.shape[0]
    left_ref[:rows, :] = upper_ref[...]
    acc_ref[:, :rows] = part_ref[...]
    set_left(half_ref, 0, [(buddy_ref, 0), (buddy_ref, span_of(*sizes))], sizes)
    left_ref[rows:, :] = half_ref[...]
    sum_ref[...] = jnp.zeros_like(sum_ref)

    @pl.when(lax.axis_index("row") % 2 == 1)
    def _():
        accumulate(half_ref, own_ref, sum_ref, sizes, tall)
        accumulate(half_ref, mate_ref, sum_ref, sizes, tall)

    acc_ref[:, rows:] = sum_ref[...]


def add_kernel(sizes, tall, left_ref, part_ref, *refs):
    *block_refs, acc_ref = refs
    acc_ref[...] = part_ref[...]
    for block_ref in block_refs:
        accumulate(left_ref, block_ref, acc_ref, sizes, tall)


def last_kernel(sizes, tall, left_ref, part_ref, *refs):
    *block_refs, out_ref, acc_ref = refs
    add_kernel(sizes, tall, left_ref, part_ref, *block_refs, acc_ref)
    write_product(out_ref, acc_ref[AUX:, :], acc_ref[ONE : ONE + 1, :])


def write_product(out_ref, product, degree):
    rows = product.shape[1]
    out_ref[:, :rows] = product
    piece = rows // AUX
    out_ref[:, rows:] = place_rows([degree[:, i * piece : (i + 1) * piece] for i in range(AUX)], piece)


def read_product(ref, segments):
    rows = ref.shape[1] * AUX // (AUX + 1)
    tail = ref[:, rows:]
    degree = jnp.concatenate([tail[i : i + 1] for i in range(AUX)], axis=1)
    size = rows // len(segments)
    pick = lambda x: jnp.concatenate([x[:, i * size : (i + 1) * size] for i in segments], axis=1)
    return pick(ref[:, :rows]), pick(degree)


def chip_kernel(mine_ref, other_ref, out_ref):
    mine, other = read_product(mine_ref, (0, 1, 2, 3)), read_product(other_ref, (1, 0, 3, 2))
    write_product(out_ref, mine[0] + other[0], mine[1] + other[1])


def join_kernel(*refs):
    *block_refs, out_ref = refs
    at = 0
    for block_ref in block_refs:
        out_ref[:, at : at + block_ref.shape[1]] = block_ref[...]
        at += block_ref.shape[1]


def update_kernel(mine_ref, other_ref, update_ref, gram_ref):
    mine, other = read_product(mine_ref, (0, 1)), read_product(other_ref, (1, 0))
    update = (mine[0] + other[0]) / (mine[1] + other[1])
    update_ref[...] = update[:, : update_ref.shape[1]]
    column = lax.broadcasted_iota(jnp.int32, gram_ref.shape, 1)
    gram = jnp.zeros(gram_ref.shape, F32)
    for k in range(update.shape[0]):
        gram = jnp.where(column == k, jnp.sum(update * update[k : k + 1], axis=1, keepdims=True), gram)
    gram_ref[...] = gram


def line_kernel(update_ref, *refs):
    *gram_refs, line_ref, out_ref = refs
    local = update_ref.shape[1] // 2
    line = functools.reduce(lambda a, b: a + b, [ref[...] for ref in gram_refs])
    line_ref[...] = line
    out_ref[:, :local] = update_ref[:, local:]
    out_ref[:, local:] = line


def basis_kernel(root, update_ref, line_ref, given_ref, *refs):
    *line_refs, out_ref = refs
    local = out_ref.shape[1]
    odd = lax.axis_index("row") % 2 == 1
    others = len(line_refs) // 2
    lines = [line_ref[...], *[ref[...] for ref in line_refs[:others]]]
    lines_given = [given_ref[:, local:], *[ref[...] for ref in line_refs[others:]]]
    gram = functools.reduce(
        lambda a, b: a + b, [jnp.where(odd, mine, given) for mine, given in zip(lines, lines_given)]
    )
    rest = jnp.where(odd, update_ref[:, :local], given_ref[:, :local])
    kvec = rest.shape[0]
    row = lax.broadcasted_iota(jnp.int32, gram.shape, 0)
    column = lax.broadcasted_iota(jnp.int32, gram.shape, 1)
    for k in range(kvec - 1):
        factor = jnp.where(row[:, :1] > k, gram[:, k : k + 1] / gram[k : k + 1, k : k + 1], F32(0))
        rest = rest - factor * rest[k : k + 1]
        gram = gram - factor * gram[k : k + 1]
    pivot = jnp.sum(jnp.where(row == column, gram, F32(0)), axis=1, keepdims=True)
    out_ref[...] = rest * (root / jnp.sqrt(pivot))


def partners(count, step):
    if count & (count - 1) == 0:
        return [i ^ step for i in range(count)]
    return [(i + step) % count for i in range(count)]


def step(points, spread, vectors):
    n_row, n_col = lax.axis_size("row"), lax.axis_size("col")
    dims, local = points.shape
    kvec = vectors.shape[0]
    packed = dims + AUX + kvec
    sizes = (dims, kvec, local)
    span = span_of(*sizes)

    def to_mate(x):
        return lax.ppermute(x, "row", [(i, i ^ 1) for i in range(n_row)])

    def along(x):
        return [lax.ppermute(x, "col", list(enumerate(partners(n_col, step)))) for step in range(1, n_col)]

    def to_buddy(x):
        return lax.ppermute(x, "row", [(i, i ^ 2) for i in range(n_row)])

    def across(x):
        return [
            lax.ppermute(
                x, "row", [(4 * i + k, 4 * j + k) for i, j in enumerate(partners(n_row // 4, step)) for k in range(4)]
            )
            for step in range(1, n_row // 4)
        ]

    def odd_only(x, places, idle):
        flat = lambda i, j: i * n_col + j
        pairs = [
            (flat(i, j), flat(*(places(i, j) if i % 2 else (i ^ idle, j)))) for i in range(n_row) for j in range(n_col)
        ]
        return lax.ppermute(x, ("row", "col"), pairs)

    def odd_along(x):
        return [odd_only(x, lambda i, j: (i, partners(n_col, step)[j]), 2) for step in range(1, n_col)]

    def odd_across(x, flip):
        others = range(1, n_row // 4)
        place = lambda i, step: 4 * partners(n_row // 4, step)[i // 4] + (i % 4 ^ flip)
        return [lax.ppermute(x, "row", [(i, place(i, step)) for i in range(n_row)]) for step in others]

    def odd_buddy(x):
        return odd_only(x, lambda i, j: (i ^ 2, j), 4 if n_row % 8 == 0 else 2)

    shape = jax.ShapeDtypeStruct
    block = call(pack_kernel, shape((AUX, span), BF16), points, spread, vectors, in_hbm=True)
    column = along(block)
    mate = to_mate(block)
    beside = across(block)
    buddy = to_buddy(call(join_kernel, shape((AUX, 2 * span), BF16), block, mate))
    rows = 4 * local
    tall = math.gcd(2 * local, 1024)
    product = shape((kvec, rows // AUX * (AUX + 1)), F32)

    def size(blocks, share=1):
        pairs = rows // share * blocks * local
        return dict(flops=2 * 2 * pairs * 160, exps=pairs, moved=10**6)

    left, part = call(
        functools.partial(own_kernel, sizes, tall),
        (shape((rows // 2, 4 * packed), BF16), shape((packed - dims, rows // 2), F32)),
        block, mate, **size(1, 2),
    )
    column, left, part = lax.optimization_barrier((column, left, part))
    joined = call(join_kernel, shape((AUX, span * (n_col - 1)), BF16), *column)
    far = across(joined)
    left, part = call(
        functools.partial(buddy_kernel, sizes, tall),
        (shape((rows, 4 * packed), BF16), shape((packed - dims, rows), F32)),
        block, mate, buddy, left, part,
        scratch=[pltpu.VMEM((rows // 2, 4 * packed), BF16), pltpu.VMEM((packed - dims, rows // 2), F32)],
        **size(1, 2),
    )
    part = call(
        functools.partial(add_kernel, sizes, tall),
        shape((packed - dims, rows), F32), left, part, *column, **size(len(column)),
    )
    rest = [*beside, *far[::-1]]
    part = call(
        functools.partial(last_kernel, sizes, tall),
        product, left, part, *rest,
        scratch=[pltpu.VMEM((packed - dims, rows), F32)], **size(len(beside) + len(far) * (n_col - 1)),
    )
    chip = call(chip_kernel, product, part, to_mate(part))
    update, gram = call(update_kernel, (shape((kvec, 2 * local), F32), shape((kvec, 128), F32)), chip, odd_buddy(chip))
    line, given = call(
        line_kernel,
        (shape(gram.shape, F32), shape((kvec, local + 128), F32)),
        update, gram, *odd_along(gram),
    )
    lines = [*odd_across(line, 0), *odd_across(line, 1)]
    root = math.sqrt(local * n_row * n_col)
    return call(
        functools.partial(basis_kernel, root),
        shape((kvec, local), F32),
        update, line, to_mate(given), *lines,
        out_vmem=False,
    )


def solution(mesh):
    in_specs = (P(None, ("row", "col")), P(("row", "col")), P(None, ("row", "col")))
    out_specs = P(None, ("row", "col"))
    return jax.shard_map(step, mesh=mesh, in_specs=in_specs, out_specs=out_specs, check_vma=False)
```

```python
import functools
import math

import jax
import jax.numpy as jnp
from jax import lax
from jax.experimental import pallas as pl
from jax.experimental.pallas import tpu as pltpu
from jax.sharding import PartitionSpec as P


VMEM = pl.BlockSpec(memory_space=pltpu.VMEM)
F32 = jnp.float32
BF16 = jnp.bfloat16
AUX = 8
ONE, SCALE = 3, 4


def call(kernel, out_shape, *args, scratch=(), out_vmem=True, in_hbm=False, flops=10**6, moved=10**5, exps=0, limit=16 * 2**20):
    return pl.pallas_call(
        kernel,
        out_shape=jax.tree.map(lambda s: pltpu.VMEM(s.shape, s.dtype), out_shape) if out_vmem else out_shape,
        in_specs=[VMEM] * len(args),
        out_specs=jax.tree.map(lambda _: VMEM, out_shape),
        scratch_shapes=scratch,
        cost_estimate=pl.CostEstimate(flops=flops, bytes_accessed=moved, transcendentals=exps),
        compiler_params=pltpu.CompilerParams(vmem_limit_bytes=limit),
    )(*[pltpu.with_memory_space_constraint(x, pltpu.HBM if in_hbm else pltpu.VMEM) for x in args])


def three_parts(x):
    hi = x.astype(BF16).astype(F32)
    rest = x - hi
    mid = rest.astype(BF16).astype(F32)
    return hi, mid, rest - mid


def span_of(dims, kvec, local):
    return (dims + kvec) // AUX * local + 128 * (-(-local // (128 * AUX)))


def pack_kernel(points_ref, spread_ref, vectors_ref, out_ref):
    local = points_ref.shape[1]
    at = 0
    for ref in (points_ref, vectors_ref):
        for top in range(0, ref.shape[0], AUX):
            out_ref[:, at : at + local] = ref[top : top + AUX, :]
            at += local
    spread = spread_ref[...].reshape(1, local).astype(F32)
    for column in range(0, local, 128 * AUX):
        pieces = [spread[:, i : i + 128] for i in range(column, min(local, column + 128 * AUX), 128)]
        out_ref[:, at : at + 128] = place_rows(pieces, 128).astype(BF16)
        at += 128


def place_rows(entries, width):
    row = lax.broadcasted_iota(jnp.int32, (AUX, width), 0)
    out = jnp.ones((AUX, width), F32)
    for place, entry in enumerate(entries):
        out = jnp.where(row == place, entry, out)
    return out


def expand(ref, at, dims, kvec, local):
    groups = [
        ref[:, pl.ds(at + i * local, local)].astype(F32) for i in range((dims + kvec) // AUX)
    ]
    points = jnp.concatenate(groups[: dims // AUX], axis=0)
    base = at + len(groups) * local
    spread = []
    for i in range(local // 128):
        tile = ref[:, pl.ds(base + i // AUX * 128, 128)].astype(F32)
        spread.append(tile[i % AUX : i % AUX + 1])
    norm = jnp.sum(points * points, axis=0, keepdims=True)
    aux = place_rows((*three_parts(norm), jnp.ones_like(norm), jnp.concatenate(spread, axis=1)), local)
    return jnp.concatenate([points, aux, *groups[dims // AUX :]], axis=0)


def left_factor(rows, dims):
    at = lambda i: rows[dims + i : dims + i + 1]
    rate = F32(math.log2(math.e)) / at(SCALE)
    norm = at(0) + at(1) + at(2)
    row = lax.broadcasted_iota(jnp.int32, (AUX, rows.shape[1]), 0)
    aux = jnp.where(row < ONE, -rate, jnp.where(row == ONE, -norm * rate, F32(0)))
    factor = jnp.concatenate(
        [2 * rate * rows[:dims], aux, jnp.zeros((rows.shape[0] - dims - AUX, rows.shape[1]), F32)], axis=0
    )
    return jnp.concatenate(three_parts(factor), axis=0)


def accumulate(left_ref, block_ref, acc_ref, sizes, tall, top=0):
    dims, _, local = sizes
    rows, span = left_ref.shape[1], span_of(*sizes)
    count = block_ref.shape[1] // span

    def step(c, carry):
        full = expand(block_ref, pl.multiple_of(c * span, 128), *sizes)
        rate = 1.0 / full[dims + SCALE : dims + SCALE + 1]
        depth = 3 * full.shape[0]
        turned = jnp.concatenate([full] * 3 + [jnp.broadcast_to(rate, (128 - depth, local))], axis=0).T
        right = turned[:, :depth].astype(BF16)
        rate = jnp.concatenate([jnp.broadcast_to(turned[:, depth : depth + 1], (local, 128))] * (tall // 128), axis=1)
        block = full[dims:].astype(BF16)
        for m in range(top, rows, tall):
            exponent = jnp.dot(right, left_ref[:, m : m + tall], preferred_element_type=F32)
            affinity = jnp.exp2(exponent * rate).astype(BF16)
            acc_ref[:, m : m + tall] += jnp.dot(block, affinity, preferred_element_type=F32)
        return carry

    if count == 1:
        step(0, 0)
    else:
        lax.fori_loop(0, count, step, 0, unroll=min(count, 3))


def set_left(left_ref, at, block_refs, sizes):
    dims, _, local = sizes
    for ref, start in block_refs:
        factor = left_factor(expand(ref, start, *sizes), dims)
        left_ref[:, at : at + local] = factor.astype(BF16)
        at += local


def own_kernel(sizes, tall, own_ref, mate_ref, left_ref, acc_ref):
    set_left(left_ref, 0, [(own_ref, 0), (mate_ref, 0)], sizes)
    acc_ref[...] = jnp.zeros_like(acc_ref)
    accumulate(left_ref, own_ref, acc_ref, sizes, tall)


def buddy_kernel(sizes, tall, own_ref, mate_ref, buddy_ref, upper_ref, part_ref, left_ref, acc_ref, half_ref, sum_ref):
    rows = upper_ref.shape[1]
    left_ref[:, :rows] = upper_ref[...]
    acc_ref[:, :rows] = part_ref[...]
    set_left(half_ref, 0, [(buddy_ref, 0), (buddy_ref, span_of(*sizes))], sizes)
    left_ref[:, rows:] = half_ref[...]
    sum_ref[...] = jnp.zeros_like(sum_ref)

    @pl.when(lax.axis_index("row") % 2 == 1)
    def _():
        accumulate(half_ref, own_ref, sum_ref, sizes, tall)
        accumulate(half_ref, mate_ref, sum_ref, sizes, tall)

    acc_ref[:, rows:] = sum_ref[...]


def add_kernel(sizes, tall, left_ref, part_ref, *refs):
    *block_refs, acc_ref = refs
    acc_ref[...] = part_ref[...]
    for block_ref in block_refs:
        accumulate(left_ref, block_ref, acc_ref, sizes, tall)


def near_kernel(sizes, tall, left_ref, part_ref, early_ref, *refs):
    *block_refs, acc_ref = refs
    add_kernel(sizes, tall, left_ref, part_ref, *block_refs, acc_ref)
    accumulate(left_ref, early_ref, acc_ref, sizes, tall, left_ref.shape[1] // 2)


def last_kernel(sizes, tall, left_ref, part_ref, *refs):
    *block_refs, out_ref, acc_ref = refs
    add_kernel(sizes, tall, left_ref, part_ref, *block_refs, acc_ref)
    write_product(out_ref, acc_ref[AUX:, :], acc_ref[ONE : ONE + 1, :])


def write_product(out_ref, product, degree):
    rows = product.shape[1]
    out_ref[:, :rows] = product
    piece = rows // AUX
    out_ref[:, rows:] = place_rows([degree[:, i * piece : (i + 1) * piece] for i in range(AUX)], piece)


def read_product(ref, segments):
    rows = ref.shape[1] * AUX // (AUX + 1)
    tail = ref[:, rows:]
    degree = jnp.concatenate([tail[i : i + 1] for i in range(AUX)], axis=1)
    size = rows // len(segments)
    pick = lambda x: jnp.concatenate([x[:, i * size : (i + 1) * size] for i in segments], axis=1)
    return pick(ref[:, :rows]), pick(degree)


def chip_kernel(mine_ref, other_ref, out_ref):
    mine, other = read_product(mine_ref, (0, 1, 2, 3)), read_product(other_ref, (1, 0, 3, 2))
    write_product(out_ref, mine[0] + other[0], mine[1] + other[1])


def join_kernel(*refs):
    *block_refs, out_ref = refs
    at = 0
    for block_ref in block_refs:
        out_ref[:, at : at + block_ref.shape[1]] = block_ref[...]
        at += block_ref.shape[1]


def update_kernel(mine_ref, other_ref, update_ref, gram_ref):
    mine, other = read_product(mine_ref, (0, 1)), read_product(other_ref, (1, 0))
    update = (mine[0] + other[0]) / (mine[1] + other[1])
    update_ref[...] = update[:, : update_ref.shape[1]]
    column = lax.broadcasted_iota(jnp.int32, gram_ref.shape, 1)
    gram = jnp.zeros(gram_ref.shape, F32)
    for k in range(update.shape[0]):
        gram = jnp.where(column == k, jnp.sum(update * update[k : k + 1], axis=1, keepdims=True), gram)
    gram_ref[...] = gram


def line_kernel(update_ref, *refs):
    *gram_refs, line_ref, out_ref = refs
    local = update_ref.shape[1] // 2
    line = functools.reduce(lambda a, b: a + b, [ref[...] for ref in gram_refs])
    line_ref[...] = line
    out_ref[:, :local] = update_ref[:, local:]
    out_ref[:, local:] = line


def basis_kernel(root, update_ref, line_ref, given_ref, *refs):
    *line_refs, out_ref = refs
    local = out_ref.shape[1]
    odd = lax.axis_index("row") % 2 == 1
    others = len(line_refs) // 2
    lines = [line_ref[...], *[ref[...] for ref in line_refs[:others]]]
    lines_given = [given_ref[:, local:], *[ref[...] for ref in line_refs[others:]]]
    gram = functools.reduce(
        lambda a, b: a + b, [jnp.where(odd, mine, given) for mine, given in zip(lines, lines_given)]
    )
    rest = jnp.where(odd, update_ref[:, :local], given_ref[:, :local])
    kvec = rest.shape[0]
    row = lax.broadcasted_iota(jnp.int32, gram.shape, 0)
    column = lax.broadcasted_iota(jnp.int32, gram.shape, 1)
    for k in range(kvec - 1):
        factor = jnp.where(row[:, :1] > k, gram[:, k : k + 1] / gram[k : k + 1, k : k + 1], F32(0))
        rest = rest - factor * rest[k : k + 1]
        gram = gram - factor * gram[k : k + 1]
    pivot = jnp.sum(jnp.where(row == column, gram, F32(0)), axis=1, keepdims=True)
    out_ref[...] = rest * (root / jnp.sqrt(pivot))


def partners(count, step):
    if count & (count - 1) == 0:
        return [i ^ step for i in range(count)]
    return [(i + step) % count for i in range(count)]


def step(points, spread, vectors):
    n_row, n_col = lax.axis_size("row"), lax.axis_size("col")
    dims, local = points.shape
    kvec = vectors.shape[0]
    packed = dims + AUX + kvec
    sizes = (dims, kvec, local)
    span = span_of(*sizes)

    def to_mate(x):
        return lax.ppermute(x, "row", [(i, i ^ 1) for i in range(n_row)])

    def along(x):
        return [lax.ppermute(x, "col", list(enumerate(partners(n_col, step)))) for step in range(1, n_col)]

    def to_buddy(x):
        return lax.ppermute(x, "row", [(i, i ^ 2) for i in range(n_row)])

    def across(x):
        return [
            lax.ppermute(
                x, "row", [(4 * i + k, 4 * j + k) for i, j in enumerate(partners(n_row // 4, step)) for k in range(4)]
            )
            for step in range(1, n_row // 4)
        ]

    def odd_only(x, places, idle):
        flat = lambda i, j: i * n_col + j
        pairs = [
            (flat(i, j), flat(*(places(i, j) if i % 2 else (i ^ idle, j)))) for i in range(n_row) for j in range(n_col)
        ]
        return lax.ppermute(x, ("row", "col"), pairs)

    def odd_along(x):
        return [odd_only(x, lambda i, j: (i, partners(n_col, step)[j]), 2) for step in range(1, n_col)]

    def odd_across(x, flip):
        others = range(1, n_row // 4)
        place = lambda i, step: 4 * partners(n_row // 4, step)[i // 4] + (i % 4 ^ flip)
        return [lax.ppermute(x, "row", [(i, place(i, step)) for i in range(n_row)]) for step in others]

    def odd_buddy(x):
        return odd_only(x, lambda i, j: (i ^ 2, j), 4 if n_row % 8 == 0 else 2)

    shape = jax.ShapeDtypeStruct
    block = call(pack_kernel, shape((AUX, span), BF16), points, spread, vectors, in_hbm=True)
    column = along(block)
    mate = to_mate(block)
    beside = across(block)
    buddy = to_buddy(call(join_kernel, shape((AUX, 2 * span), BF16), block, mate))
    rows = 4 * local
    tall = math.gcd(2 * local, 1024)
    product = shape((kvec, rows // AUX * (AUX + 1)), F32)

    def size(blocks, share=1):
        pairs = rows // share * blocks * local
        return dict(flops=2 * 2 * pairs * 160, exps=pairs, moved=10**6)

    left, part = call(
        functools.partial(own_kernel, sizes, tall),
        (shape((3 * packed, rows // 2), BF16), shape((packed - dims, rows // 2), F32)),
        block, mate, **size(1, 2),
    )
    middle = n_col // 2 - 1
    early, later = column[middle], column[:middle] + column[middle + 1 :]
    part = call(
        functools.partial(add_kernel, sizes, tall),
        shape((packed - dims, rows // 2), F32), left, part, early, **size(1, 2),
    )
    later, left, part = lax.optimization_barrier((later, left, part))
    joined = call(join_kernel, shape((AUX, span * (n_col - 1)), BF16), early, *later)
    far = across(joined)
    left, part = call(
        functools.partial(buddy_kernel, sizes, tall),
        (shape((3 * packed, rows), BF16), shape((packed - dims, rows), F32)),
        block, mate, buddy, left, part,
        scratch=[pltpu.VMEM((3 * packed, rows // 2), BF16), pltpu.VMEM((packed - dims, rows // 2), F32)],
        **size(1, 2),
    )
    part = call(
        functools.partial(near_kernel, sizes, tall),
        shape((packed - dims, rows), F32), left, part, early, *later, **size(len(column)),
    )
    part = call(
        functools.partial(add_kernel, sizes, tall),
        shape((packed - dims, rows), F32), left, part, *beside, **size(len(beside)),
    )
    part = call(
        functools.partial(last_kernel, sizes, tall),
        product, left, part, *far[::-1],
        scratch=[pltpu.VMEM((packed - dims, rows), F32)], **size(len(far) * (n_col - 1)),
    )
    chip = call(chip_kernel, product, part, to_mate(part))
    update, gram = call(update_kernel, (shape((kvec, 2 * local), F32), shape((kvec, 128), F32)), chip, odd_buddy(chip))
    line, given = call(
        line_kernel,
        (shape(gram.shape, F32), shape((kvec, local + 128), F32)),
        update, gram, *odd_along(gram),
    )
    lines = [*odd_across(line, 0), *odd_across(line, 1)]
    root = math.sqrt(local * n_row * n_col)
    return call(
        functools.partial(basis_kernel, root),
        shape((kvec, local), F32),
        update, line, to_mate(given), *lines,
        out_vmem=False,
    )


def solution(mesh):
    in_specs = (P(None, ("row", "col")), P(("row", "col")), P(None, ("row", "col")))
    out_specs = P(None, ("row", "col"))
    return jax.shard_map(step, mesh=mesh, in_specs=in_specs, out_specs=out_specs, check_vma=False)
```

```python
import functools
import math

import jax
import jax.numpy as jnp
from jax import lax
from jax.experimental import pallas as pl
from jax.experimental.pallas import tpu as pltpu
from jax.sharding import PartitionSpec as P


VMEM = pl.BlockSpec(memory_space=pltpu.VMEM)
F32 = jnp.float32
BF16 = jnp.bfloat16
AUX = 8
ONE, SCALE = 3, 4


def call(kernel, out_shape, *args, scratch=(), out_vmem=True, in_hbm=False, flops=10**6, moved=10**5, exps=0, limit=16 * 2**20):
    return pl.pallas_call(
        kernel,
        out_shape=jax.tree.map(lambda s: pltpu.VMEM(s.shape, s.dtype), out_shape) if out_vmem else out_shape,
        in_specs=[VMEM] * len(args),
        out_specs=jax.tree.map(lambda _: VMEM, out_shape),
        scratch_shapes=scratch,
        cost_estimate=pl.CostEstimate(flops=flops, bytes_accessed=moved, transcendentals=exps),
        compiler_params=pltpu.CompilerParams(vmem_limit_bytes=limit),
    )(*[pltpu.with_memory_space_constraint(x, pltpu.HBM if in_hbm else pltpu.VMEM) for x in args])


def three_parts(x):
    hi = x.astype(BF16).astype(F32)
    rest = x - hi
    mid = rest.astype(BF16).astype(F32)
    return hi, mid, rest - mid


def span_of(dims, kvec, local):
    return (dims + kvec) // AUX * local + 128 * (-(-local // (128 * AUX)))


def pack_kernel(points_ref, spread_ref, vectors_ref, out_ref):
    local = points_ref.shape[1]
    at = 0
    for ref in (points_ref, vectors_ref):
        for top in range(0, ref.shape[0], AUX):
            out_ref[:, at : at + local] = ref[top : top + AUX, :]
            at += local
    spread = spread_ref[...].reshape(1, local).astype(F32)
    for column in range(0, local, 128 * AUX):
        pieces = [spread[:, i : i + 128] for i in range(column, min(local, column + 128 * AUX), 128)]
        out_ref[:, at : at + 128] = place_rows(pieces, 128).astype(BF16)
        at += 128


def place_rows(entries, width):
    row = lax.broadcasted_iota(jnp.int32, (AUX, width), 0)
    out = jnp.ones((AUX, width), F32)
    for place, entry in enumerate(entries):
        out = jnp.where(row == place, entry, out)
    return out


def expand(ref, at, dims, kvec, local):
    groups = [
        ref[:, pl.ds(at + i * local, local)].astype(F32) for i in range((dims + kvec) // AUX)
    ]
    points = jnp.concatenate(groups[: dims // AUX], axis=0)
    base = at + len(groups) * local
    spread = []
    for i in range(local // 128):
        tile = ref[:, pl.ds(base + i // AUX * 128, 128)].astype(F32)
        spread.append(tile[i % AUX : i % AUX + 1])
    norm = jnp.sum(points * points, axis=0, keepdims=True)
    aux = place_rows((*three_parts(norm), jnp.ones_like(norm), jnp.concatenate(spread, axis=1)), local)
    return jnp.concatenate([points, aux, *groups[dims // AUX :]], axis=0)


def left_factor(rows, dims):
    at = lambda i: rows[dims + i : dims + i + 1]
    rate = F32(math.log2(math.e)) / at(SCALE)
    norm = at(0) + at(1) + at(2)
    row = lax.broadcasted_iota(jnp.int32, (AUX, rows.shape[1]), 0)
    aux = jnp.where(row < ONE, -rate, jnp.where(row == ONE, -norm * rate, F32(0)))
    factor = jnp.concatenate(
        [2 * rate * rows[:dims], aux, jnp.zeros((rows.shape[0] - dims - AUX, rows.shape[1]), F32)], axis=0
    )
    return jnp.concatenate(three_parts(factor), axis=0)


def accumulate(left_ref, block_ref, acc_ref, sizes, tall, top=0):
    dims, _, local = sizes
    rows, span = left_ref.shape[1], span_of(*sizes)
    count = block_ref.shape[1] // span

    def step(c, carry):
        full = expand(block_ref, pl.multiple_of(c * span, 128), *sizes)
        rate = 1.0 / full[dims + SCALE : dims + SCALE + 1]
        depth = 3 * full.shape[0]
        turned = jnp.concatenate([full] * 3 + [jnp.broadcast_to(rate, (128 - depth, local))], axis=0).T
        right = turned[:, :depth].astype(BF16)
        rate = jnp.concatenate([jnp.broadcast_to(turned[:, depth : depth + 1], (local, 128))] * (tall // 128), axis=1)
        block = full[dims:].astype(BF16)
        for m in range(top, rows, tall):
            exponent = jnp.dot(right, left_ref[:, m : m + tall], preferred_element_type=F32)
            affinity = jnp.exp2(exponent * rate).astype(BF16)
            acc_ref[:, m : m + tall] += jnp.dot(block, affinity, preferred_element_type=F32)
        return carry

    if count == 1:
        step(0, 0)
    else:
        lax.fori_loop(0, count, step, 0, unroll=min(count, 3))


def set_left(left_ref, at, block_refs, sizes):
    dims, _, local = sizes
    for ref, start in block_refs:
        factor = left_factor(expand(ref, start, *sizes), dims)
        left_ref[:, at : at + local] = factor.astype(BF16)
        at += local


def own_kernel(sizes, tall, own_ref, mate_ref, left_ref, acc_ref):
    set_left(left_ref, 0, [(own_ref, 0), (mate_ref, 0)], sizes)
    acc_ref[...] = jnp.zeros_like(acc_ref)
    accumulate(left_ref, own_ref, acc_ref, sizes, tall)


def buddy_kernel(sizes, tall, own_ref, mate_ref, buddy_ref, upper_ref, part_ref, left_ref, acc_ref, half_ref, sum_ref):
    rows = upper_ref.shape[1]
    left_ref[:, :rows] = upper_ref[...]
    acc_ref[:, :rows] = part_ref[...]
    set_left(half_ref, 0, [(buddy_ref, 0), (buddy_ref, span_of(*sizes))], sizes)
    left_ref[:, rows:] = half_ref[...]
    sum_ref[...] = jnp.zeros_like(sum_ref)

    @pl.when(lax.axis_index("row") % 2 == 1)
    def _():
        accumulate(half_ref, own_ref, sum_ref, sizes, tall)
        accumulate(half_ref, mate_ref, sum_ref, sizes, tall)

    acc_ref[:, rows:] = sum_ref[...]


def add_kernel(sizes, tall, left_ref, part_ref, *refs):
    *block_refs, acc_ref = refs
    acc_ref[...] = part_ref[...]
    for block_ref in block_refs:
        accumulate(left_ref, block_ref, acc_ref, sizes, tall)


def near_kernel(sizes, tall, left_ref, part_ref, early_ref, *refs):
    *block_refs, acc_ref = refs
    add_kernel(sizes, tall, left_ref, part_ref, *block_refs, acc_ref)
    accumulate(left_ref, early_ref, acc_ref, sizes, tall, left_ref.shape[1] // 2)


def last_kernel(sizes, tall, left_ref, part_ref, *refs):
    *block_refs, out_ref, acc_ref = refs
    add_kernel(sizes, tall, left_ref, part_ref, *block_refs, acc_ref)
    write_product(out_ref, acc_ref[AUX:, :], acc_ref[ONE : ONE + 1, :])


def write_product(out_ref, product, degree):
    rows = product.shape[1]
    out_ref[:, :rows] = product
    piece = rows // AUX
    out_ref[:, rows:] = place_rows([degree[:, i * piece : (i + 1) * piece] for i in range(AUX)], piece)


def read_product(ref, segments):
    rows = ref.shape[1] * AUX // (AUX + 1)
    tail = ref[:, rows:]
    degree = jnp.concatenate([tail[i : i + 1] for i in range(AUX)], axis=1)
    size = rows // len(segments)
    pick = lambda x: jnp.concatenate([x[:, i * size : (i + 1) * size] for i in segments], axis=1)
    return pick(ref[:, :rows]), pick(degree)


def chip_kernel(mine_ref, other_ref, out_ref):
    mine, other = read_product(mine_ref, (0, 1, 2, 3)), read_product(other_ref, (1, 0, 3, 2))
    write_product(out_ref, mine[0] + other[0], mine[1] + other[1])


def join_kernel(*refs):
    *block_refs, out_ref = refs
    at = 0
    for block_ref in block_refs:
        out_ref[:, at : at + block_ref.shape[1]] = block_ref[...]
        at += block_ref.shape[1]


def update_kernel(mine_ref, other_ref, update_ref, gram_ref):
    mine, other = read_product(mine_ref, (0, 1)), read_product(other_ref, (1, 0))
    update = (mine[0] + other[0]) / (mine[1] + other[1])
    update_ref[...] = update[:, : update_ref.shape[1]]
    column = lax.broadcasted_iota(jnp.int32, gram_ref.shape, 1)
    gram = jnp.zeros(gram_ref.shape, F32)
    for k in range(update.shape[0]):
        gram = jnp.where(column == k, jnp.sum(update * update[k : k + 1], axis=1, keepdims=True), gram)
    gram_ref[...] = gram


def line_kernel(update_ref, *refs):
    *gram_refs, line_ref, out_ref = refs
    local = update_ref.shape[1] // 2
    line = functools.reduce(lambda a, b: a + b, [ref[...] for ref in gram_refs])
    line_ref[...] = line
    out_ref[:, :local] = update_ref[:, local:]
    out_ref[:, local:] = line


def basis_kernel(root, update_ref, line_ref, given_ref, *refs):
    *line_refs, out_ref = refs
    local = out_ref.shape[1]
    odd = lax.axis_index("row") % 2 == 1
    others = len(line_refs) // 2
    lines = [line_ref[...], *[ref[...] for ref in line_refs[:others]]]
    lines_given = [given_ref[:, local:], *[ref[...] for ref in line_refs[others:]]]
    gram = functools.reduce(
        lambda a, b: a + b, [jnp.where(odd, mine, given) for mine, given in zip(lines, lines_given)]
    )
    rest = jnp.where(odd, update_ref[:, :local], given_ref[:, :local])
    kvec = rest.shape[0]
    row = lax.broadcasted_iota(jnp.int32, gram.shape, 0)
    spread_out = lambda x: jnp.concatenate([x] * (local // 128), axis=1)
    columns = [jnp.broadcast_to(gram[:, k : k + 1], gram.shape) for k in range(kvec)]
    pivot = columns[0]
    for k in range(kvec):
        pivot = jnp.where(row == k, columns[k], pivot)
        factor = jnp.where(row > k, columns[k] / columns[k][k : k + 1], F32(0))
        for j in range(k + 1, kvec):
            columns[j] = columns[j] - factor * columns[j][k : k + 1]
        rest = rest - spread_out(factor) * rest[k : k + 1]
    out_ref[...] = rest * spread_out(root / jnp.sqrt(pivot))


def partners(count, step):
    if count & (count - 1) == 0:
        return [i ^ step for i in range(count)]
    return [(i + step) % count for i in range(count)]


def step(points, spread, vectors):
    n_row, n_col = lax.axis_size("row"), lax.axis_size("col")
    dims, local = points.shape
    kvec = vectors.shape[0]
    packed = dims + AUX + kvec
    sizes = (dims, kvec, local)
    span = span_of(*sizes)

    def to_mate(x):
        return lax.ppermute(x, "row", [(i, i ^ 1) for i in range(n_row)])

    def along(x):
        return [lax.ppermute(x, "col", list(enumerate(partners(n_col, step)))) for step in range(1, n_col)]

    def to_buddy(x):
        return lax.ppermute(x, "row", [(i, i ^ 2) for i in range(n_row)])

    def across(x):
        return [
            lax.ppermute(
                x, "row", [(4 * i + k, 4 * j + k) for i, j in enumerate(partners(n_row // 4, step)) for k in range(4)]
            )
            for step in range(1, n_row // 4)
        ]

    def odd_only(x, places, idle):
        flat = lambda i, j: i * n_col + j
        pairs = [
            (flat(i, j), flat(*(places(i, j) if i % 2 else (i ^ idle, j)))) for i in range(n_row) for j in range(n_col)
        ]
        return lax.ppermute(x, ("row", "col"), pairs)

    def odd_along(x):
        return [odd_only(x, lambda i, j: (i, partners(n_col, step)[j]), 2) for step in range(1, n_col)]

    def odd_across(x, flip):
        others = range(1, n_row // 4)
        place = lambda i, step: 4 * partners(n_row // 4, step)[i // 4] + (i % 4 ^ flip)
        return [lax.ppermute(x, "row", [(i, place(i, step)) for i in range(n_row)]) for step in others]

    def odd_buddy(x):
        return odd_only(x, lambda i, j: (i ^ 2, j), 2)

    shape = jax.ShapeDtypeStruct
    block = call(pack_kernel, shape((AUX, span), BF16), points, spread, vectors, in_hbm=True)
    column = along(block)
    mate = to_mate(block)
    beside = across(block)
    buddy = to_buddy(call(join_kernel, shape((AUX, 2 * span), BF16), block, mate))
    rows = 4 * local
    tall = math.gcd(2 * local, 1024)
    product = shape((kvec, rows // AUX * (AUX + 1)), F32)

    def size(blocks, share=1):
        pairs = rows // share * blocks * local
        return dict(flops=2 * 2 * pairs * 160, exps=pairs, moved=10**6)

    left, part = call(
        functools.partial(own_kernel, sizes, tall),
        (shape((3 * packed, rows // 2), BF16), shape((packed - dims, rows // 2), F32)),
        block, mate, **size(1, 2),
    )
    middle = n_col // 2 - 1
    early, later = column[middle], column[:middle] + column[middle + 1 :]
    part = call(
        functools.partial(add_kernel, sizes, tall),
        shape((packed - dims, rows // 2), F32), left, part, early, **size(1, 2),
    )
    later, left, part = lax.optimization_barrier((later, left, part))
    joined = call(join_kernel, shape((AUX, span * (n_col - 1)), BF16), early, *later)
    far = across(joined)
    left, part = call(
        functools.partial(buddy_kernel, sizes, tall),
        (shape((3 * packed, rows), BF16), shape((packed - dims, rows), F32)),
        block, mate, buddy, left, part,
        scratch=[pltpu.VMEM((3 * packed, rows // 2), BF16), pltpu.VMEM((packed - dims, rows // 2), F32)],
        **size(1, 2),
    )
    part = call(
        functools.partial(near_kernel, sizes, tall),
        shape((packed - dims, rows), F32), left, part, early, *later, **size(len(column)),
    )
    part = call(
        functools.partial(add_kernel, sizes, tall),
        shape((packed - dims, rows), F32), left, part, *beside, **size(len(beside)),
    )
    part = call(
        functools.partial(last_kernel, sizes, tall),
        product, left, part, *far[::-1],
        scratch=[pltpu.VMEM((packed - dims, rows), F32)], **size(len(far) * (n_col - 1)),
    )
    chip = call(chip_kernel, product, part, to_mate(part))
    update, gram = call(update_kernel, (shape((kvec, 2 * local), F32), shape((kvec, 128), F32)), chip, odd_buddy(chip))
    line, given = call(
        line_kernel,
        (shape(gram.shape, F32), shape((kvec, local + 128), F32)),
        update, gram, *odd_along(gram),
    )
    lines = [*odd_across(line, 0), *odd_across(line, 1)]
    root = math.sqrt(local * n_row * n_col)
    return call(
        functools.partial(basis_kernel, root),
        shape((kvec, local), F32),
        update, line, to_mate(given), *lines,
        out_vmem=False,
    )


def solution(mesh):
    in_specs = (P(None, ("row", "col")), P(("row", "col")), P(None, ("row", "col")))
    out_specs = P(None, ("row", "col"))
    return jax.shard_map(step, mesh=mesh, in_specs=in_specs, out_specs=out_specs, check_vma=False)
```

```python
import functools
import math

import jax
import jax.numpy as jnp
from jax import lax
from jax.experimental import pallas as pl
from jax.experimental.pallas import tpu as pltpu
from jax.sharding import PartitionSpec as P


VMEM = pl.BlockSpec(memory_space=pltpu.VMEM)
F32 = jnp.float32
BF16 = jnp.bfloat16
AUX = 8
ONE, SCALE = 3, 4


def call(kernel, out_shape, *args, scratch=(), out_vmem=True, in_hbm=False, flops=10**6, moved=10**5, exps=0, limit=16 * 2**20):
    return pl.pallas_call(
        kernel,
        out_shape=jax.tree.map(lambda s: pltpu.VMEM(s.shape, s.dtype), out_shape) if out_vmem else out_shape,
        in_specs=[VMEM] * len(args),
        out_specs=jax.tree.map(lambda _: VMEM, out_shape),
        scratch_shapes=scratch,
        cost_estimate=pl.CostEstimate(flops=flops, bytes_accessed=moved, transcendentals=exps),
        compiler_params=pltpu.CompilerParams(vmem_limit_bytes=limit),
    )(*[pltpu.with_memory_space_constraint(x, pltpu.HBM if in_hbm else pltpu.VMEM) for x in args])


def three_parts(x):
    hi = x.astype(BF16).astype(F32)
    rest = x - hi
    mid = rest.astype(BF16).astype(F32)
    return hi, mid, rest - mid


def span_of(dims, kvec, local):
    return (dims + kvec) // AUX * local + 128 * (-(-local // (128 * AUX)))


def pack_kernel(points_ref, spread_ref, vectors_ref, out_ref):
    local = points_ref.shape[1]
    at = 0
    for ref in (points_ref, vectors_ref):
        for top in range(0, ref.shape[0], AUX):
            out_ref[:, at : at + local] = ref[top : top + AUX, :]
            at += local
    spread = spread_ref[...].reshape(1, local).astype(F32)
    for column in range(0, local, 128 * AUX):
        pieces = [spread[:, i : i + 128] for i in range(column, min(local, column + 128 * AUX), 128)]
        out_ref[:, at : at + 128] = place_rows(pieces, 128).astype(BF16)
        at += 128


def place_rows(entries, width):
    row = lax.broadcasted_iota(jnp.int32, (AUX, width), 0)
    out = jnp.ones((AUX, width), F32)
    for place, entry in enumerate(entries):
        out = jnp.where(row == place, entry, out)
    return out


def expand(ref, at, dims, kvec, local):
    groups = [
        ref[:, pl.ds(at + i * local, local)].astype(F32) for i in range((dims + kvec) // AUX)
    ]
    points = jnp.concatenate(groups[: dims // AUX], axis=0)
    base = at + len(groups) * local
    spread = []
    for i in range(local // 128):
        tile = ref[:, pl.ds(base + i // AUX * 128, 128)].astype(F32)
        spread.append(tile[i % AUX : i % AUX + 1])
    norm = jnp.sum(points * points, axis=0, keepdims=True)
    aux = place_rows((*three_parts(norm), jnp.ones_like(norm), jnp.concatenate(spread, axis=1)), local)
    return jnp.concatenate([points, aux, *groups[dims // AUX :]], axis=0)


def left_factor(rows, dims):
    at = lambda i: rows[dims + i : dims + i + 1]
    rate = F32(math.log2(math.e)) / at(SCALE)
    norm = at(0) + at(1) + at(2)
    row = lax.broadcasted_iota(jnp.int32, (AUX, rows.shape[1]), 0)
    aux = jnp.where(row < ONE, -rate, jnp.where(row == ONE, -norm * rate, F32(0)))
    factor = jnp.concatenate(
        [2 * rate * rows[:dims], aux, jnp.zeros((rows.shape[0] - dims - AUX, rows.shape[1]), F32)], axis=0
    )
    return jnp.concatenate(three_parts(factor), axis=0)


def accumulate(left_ref, block_ref, acc_ref, sizes, tall, top=0):
    dims, _, local = sizes
    rows, span = left_ref.shape[1], span_of(*sizes)
    count = block_ref.shape[1] // span

    def step(c, carry):
        full = expand(block_ref, pl.multiple_of(c * span, 128), *sizes)
        rate = 1.0 / full[dims + SCALE : dims + SCALE + 1]
        depth = 3 * full.shape[0]
        rows16 = full.astype(BF16)
        right = jnp.concatenate([rows16] * 3 + [jnp.zeros((128 - depth, local), BF16)], axis=0).T[:, :depth]
        rate = jnp.concatenate([jnp.broadcast_to(rate, (128, local)).T] * (tall // 128), axis=1)
        block = full[dims:].astype(BF16)
        for m in range(top, rows, tall):
            exponent = jnp.dot(right, left_ref[:, m : m + tall], preferred_element_type=F32)
            affinity = jnp.exp2(exponent * rate).astype(BF16)
            acc_ref[:, m : m + tall] += jnp.dot(block, affinity, preferred_element_type=F32)
        return carry

    if count == 1:
        step(0, 0)
    else:
        lax.fori_loop(0, count, step, 0, unroll=min(count, 3))


def set_left(left_ref, at, block_refs, sizes):
    dims, _, local = sizes
    for ref, start in block_refs:
        factor = left_factor(expand(ref, start, *sizes), dims)
        left_ref[:, at : at + local] = factor.astype(BF16)
        at += local


def own_kernel(sizes, tall, own_ref, mate_ref, left_ref, acc_ref):
    set_left(left_ref, 0, [(own_ref, 0), (mate_ref, 0)], sizes)
    acc_ref[...] = jnp.zeros_like(acc_ref)
    accumulate(left_ref, own_ref, acc_ref, sizes, tall)


def buddy_kernel(sizes, tall, own_ref, mate_ref, buddy_ref, upper_ref, part_ref, left_ref, acc_ref, half_ref, sum_ref):
    rows = upper_ref.shape[1]
    left_ref[:, :rows] = upper_ref[...]
    acc_ref[:, :rows] = part_ref[...]
    set_left(half_ref, 0, [(buddy_ref, 0), (buddy_ref, span_of(*sizes))], sizes)
    left_ref[:, rows:] = half_ref[...]
    sum_ref[...] = jnp.zeros_like(sum_ref)

    @pl.when(lax.axis_index("row") % 2 == 1)
    def _():
        accumulate(half_ref, own_ref, sum_ref, sizes, tall)
        accumulate(half_ref, mate_ref, sum_ref, sizes, tall)

    acc_ref[:, rows:] = sum_ref[...]


def add_kernel(sizes, tall, left_ref, part_ref, *refs):
    *block_refs, acc_ref = refs
    acc_ref[...] = part_ref[...]
    for block_ref in block_refs:
        accumulate(left_ref, block_ref, acc_ref, sizes, tall)


def near_kernel(sizes, tall, left_ref, part_ref, early_ref, *refs):
    *block_refs, acc_ref = refs
    add_kernel(sizes, tall, left_ref, part_ref, *block_refs, acc_ref)
    accumulate(left_ref, early_ref, acc_ref, sizes, tall, left_ref.shape[1] // 2)


def last_kernel(sizes, tall, left_ref, part_ref, *refs):
    *block_refs, out_ref, acc_ref = refs
    add_kernel(sizes, tall, left_ref, part_ref, *block_refs, acc_ref)
    write_product(out_ref, acc_ref[AUX:, :], acc_ref[ONE : ONE + 1, :])


def write_product(out_ref, product, degree):
    rows = product.shape[1]
    out_ref[:, :rows] = product
    piece = rows // AUX
    out_ref[:, rows:] = place_rows([degree[:, i * piece : (i + 1) * piece] for i in range(AUX)], piece)


def read_product(ref, segments):
    rows = ref.shape[1] * AUX // (AUX + 1)
    tail = ref[:, rows:]
    degree = jnp.concatenate([tail[i : i + 1] for i in range(AUX)], axis=1)
    size = rows // len(segments)
    pick = lambda x: jnp.concatenate([x[:, i * size : (i + 1) * size] for i in segments], axis=1)
    return pick(ref[:, :rows]), pick(degree)


def chip_kernel(mine_ref, other_ref, out_ref):
    mine, other = read_product(mine_ref, (0, 1, 2, 3)), read_product(other_ref, (1, 0, 3, 2))
    write_product(out_ref, mine[0] + other[0], mine[1] + other[1])


def join_kernel(*refs):
    *block_refs, out_ref = refs
    at = 0
    for block_ref in block_refs:
        out_ref[:, at : at + block_ref.shape[1]] = block_ref[...]
        at += block_ref.shape[1]


def update_kernel(mine_ref, other_ref, update_ref, gram_ref):
    mine, other = read_product(mine_ref, (0, 1)), read_product(other_ref, (1, 0))
    update = (mine[0] + other[0]) / (mine[1] + other[1])
    update_ref[...] = update[:, : update_ref.shape[1]]
    column = lax.broadcasted_iota(jnp.int32, gram_ref.shape, 1)
    gram = jnp.zeros(gram_ref.shape, F32)
    for k in range(update.shape[0]):
        gram = jnp.where(column == k, jnp.sum(update * update[k : k + 1], axis=1, keepdims=True), gram)
    gram_ref[...] = gram


def line_kernel(update_ref, *refs):
    *gram_refs, line_ref, out_ref = refs
    local = update_ref.shape[1] // 2
    line = functools.reduce(lambda a, b: a + b, [ref[...] for ref in gram_refs])
    line_ref[...] = line
    out_ref[:, :local] = update_ref[:, local:]
    out_ref[:, local:] = line


def basis_kernel(root, update_ref, line_ref, given_ref, *refs):
    *line_refs, out_ref = refs
    local = out_ref.shape[1]
    odd = lax.axis_index("row") % 2 == 1
    others = len(line_refs) // 2
    lines = [line_ref[...], *[ref[...] for ref in line_refs[:others]]]
    lines_given = [given_ref[:, local:], *[ref[...] for ref in line_refs[others:]]]
    gram = functools.reduce(
        lambda a, b: a + b, [jnp.where(odd, mine, given) for mine, given in zip(lines, lines_given)]
    )
    rest = jnp.where(odd, update_ref[:, :local], given_ref[:, :local])
    kvec = rest.shape[0]
    row = lax.broadcasted_iota(jnp.int32, gram.shape, 0)
    spread_out = lambda x: jnp.concatenate([x] * (local // 128), axis=1)
    columns = [jnp.broadcast_to(gram[:, k : k + 1], gram.shape) for k in range(kvec)]
    pivot = columns[0]
    for k in range(kvec):
        pivot = jnp.where(row == k, columns[k], pivot)
        factor = jnp.where(row > k, columns[k] / columns[k][k : k + 1], F32(0))
        for j in range(k + 1, kvec):
            columns[j] = columns[j] - factor * columns[j][k : k + 1]
        rest = rest - spread_out(factor) * rest[k : k + 1]
    out_ref[...] = rest * spread_out(root / jnp.sqrt(pivot))


def partners(count, step):
    if count & (count - 1) == 0:
        return [i ^ step for i in range(count)]
    return [(i + step) % count for i in range(count)]


def step(points, spread, vectors):
    n_row, n_col = lax.axis_size("row"), lax.axis_size("col")
    dims, local = points.shape
    kvec = vectors.shape[0]
    packed = dims + AUX + kvec
    sizes = (dims, kvec, local)
    span = span_of(*sizes)

    def to_mate(x):
        return lax.ppermute(x, "row", [(i, i ^ 1) for i in range(n_row)])

    def along(x):
        return [lax.ppermute(x, "col", list(enumerate(partners(n_col, step)))) for step in range(1, n_col)]

    def to_buddy(x):
        return lax.ppermute(x, "row", [(i, i ^ 2) for i in range(n_row)])

    def across(x):
        return [
            lax.ppermute(
                x, "row", [(4 * i + k, 4 * j + k) for i, j in enumerate(partners(n_row // 4, step)) for k in range(4)]
            )
            for step in range(1, n_row // 4)
        ]

    def odd_only(x, places, idle):
        flat = lambda i, j: i * n_col + j
        pairs = [
            (flat(i, j), flat(*(places(i, j) if i % 2 else (i ^ idle, j)))) for i in range(n_row) for j in range(n_col)
        ]
        return lax.ppermute(x, ("row", "col"), pairs)

    def odd_along(x):
        return [odd_only(x, lambda i, j: (i, partners(n_col, step)[j]), 2) for step in range(1, n_col)]

    def odd_across(x, flip):
        others = range(1, n_row // 4)
        place = lambda i, step: 4 * partners(n_row // 4, step)[i // 4] + (i % 4 ^ flip)
        return [lax.ppermute(x, "row", [(i, place(i, step)) for i in range(n_row)]) for step in others]

    def odd_buddy(x):
        return odd_only(x, lambda i, j: (i ^ 2, j), 2)

    shape = jax.ShapeDtypeStruct
    block = call(pack_kernel, shape((AUX, span), BF16), points, spread, vectors, in_hbm=True)
    column = along(block)
    mate = to_mate(block)
    beside = across(block)
    buddy = to_buddy(call(join_kernel, shape((AUX, 2 * span), BF16), block, mate))
    rows = 4 * local
    tall = math.gcd(2 * local, 1024)
    product = shape((kvec, rows // AUX * (AUX + 1)), F32)

    def size(blocks, share=1):
        pairs = rows // share * blocks * local
        return dict(flops=2 * 2 * pairs * 160, exps=pairs, moved=10**6)

    left, part = call(
        functools.partial(own_kernel, sizes, tall),
        (shape((3 * packed, rows // 2), BF16), shape((packed - dims, rows // 2), F32)),
        block, mate, **size(1, 2),
    )
    middle = n_col // 2 - 1
    early, later = column[middle], column[:middle] + column[middle + 1 :]
    part = call(
        functools.partial(add_kernel, sizes, tall),
        shape((packed - dims, rows // 2), F32), left, part, early, **size(1, 2),
    )
    later, left, part = lax.optimization_barrier((later, left, part))
    joined = call(join_kernel, shape((AUX, span * (n_col - 1)), BF16), early, *later)
    far = across(joined)
    left, part = call(
        functools.partial(buddy_kernel, sizes, tall),
        (shape((3 * packed, rows), BF16), shape((packed - dims, rows), F32)),
        block, mate, buddy, left, part,
        scratch=[pltpu.VMEM((3 * packed, rows // 2), BF16), pltpu.VMEM((packed - dims, rows // 2), F32)],
        **size(1, 2),
    )
    part = call(
        functools.partial(near_kernel, sizes, tall),
        shape((packed - dims, rows), F32), left, part, early, *later, **size(len(column)),
    )
    part = call(
        functools.partial(add_kernel, sizes, tall),
        shape((packed - dims, rows), F32), left, part, *beside, **size(len(beside)),
    )
    part = call(
        functools.partial(last_kernel, sizes, tall),
        product, left, part, *far[::-1],
        scratch=[pltpu.VMEM((packed - dims, rows), F32)], **size(len(far) * (n_col - 1)),
    )
    chip = call(chip_kernel, product, part, to_mate(part))
    update, gram = call(update_kernel, (shape((kvec, 2 * local), F32), shape((kvec, 128), F32)), chip, odd_buddy(chip))
    line, given = call(
        line_kernel,
        (shape(gram.shape, F32), shape((kvec, local + 128), F32)),
        update, gram, *odd_along(gram),
    )
    lines = [*odd_across(line, 0), *odd_across(line, 1)]
    root = math.sqrt(local * n_row * n_col)
    return call(
        functools.partial(basis_kernel, root),
        shape((kvec, local), F32),
        update, line, to_mate(given), *lines,
        out_vmem=False,
    )


def solution(mesh):
    in_specs = (P(None, ("row", "col")), P(("row", "col")), P(None, ("row", "col")))
    out_specs = P(None, ("row", "col"))
    return jax.shard_map(step, mesh=mesh, in_specs=in_specs, out_specs=out_specs, check_vma=False)
```
